32 devices in a mesh: section: 2 (over y), expert: 8 (over z, x), dp: 2 (over core).
Axes of the slice: x: 2, y: 2, z: 4, core: 2. Of those that a mesh axis runs over, the one named last changes fastest.
Arguments:
- tokens_in: bfloat16 [8, 256, 2048], P(None, ('expert', 'dp')), may hold values from -6 to 6
- cotangent: bfloat16 [8, 256, 2048], P(None, ('expert', 'dp')), may hold values from -4 to 4
- routes: int32 [2, 8, 256, 8], P('section', None, ('expert', 'dp')), may hold values from 0 to 15, all different within a row; in each aligned block of 16 rows (0 to 15, 16 to 31, ..., all dimensions but the last counted through in order) at most 10 rows name the same one
- router_weights: float32 [2, 8, 256, 8], P('section', None, ('expert', 'dp')), may hold values from 0.1 to 0.6
- norm_gain: float32 [2, 2048], P('section'), may hold values from 0.25 to 1.75
- w_gate: bfloat16 [2, 16, 2048, 512], P('section', 'expert'), may hold values from -0.125 to 0.125
- w_up: bfloat16 [2, 16, 2048, 512], P('section', 'expert'), may hold values from -0.125 to 0.125
- w_down: bfloat16 [2, 16, 512, 2048], P('section', 'expert'), may hold values from -0.25 to 0.25
Outputs:
- layer_out: bfloat16 [2, 8, 256, 2048], P('section', None, ('expert', 'dp'))
- input_grad: bfloat16 [2, 8, 256, 2048], P('section', None, ('expert', 'dp'))
- grad_gate: bfloat16 [2, 16, 2048, 512], P('section', 'expert', 'dp')
- grad_up: bfloat16 [2, 16, 2048, 512], P('section', 'expert', 'dp')
- grad_down: bfloat16 [2, 16, 512, 2048], P('section', 'expert', 'dp')
The draws below stay inside these ranges and needn't reach their ends.
Inputs may be any that keep to these rules, and one draw needn't show every extreme that they name: `routes`: each row names 8 different experts. In each aligned block of 16 rows (the tokens of one device for one layer and one micro-batch) no expert is named by more than 10 rows, and in some blocks one is named by exactly 10.
All inputs are finite; a program needn't handle non-finite values.
Results may differ from the reference program's by a relative error of at most 0.022.
Values may be sent and summed in bfloat16 or wider, within the bound.
A program may use at most 128 MiB of HBM per device.

```python
import math
import jax
import jax.numpy as jnp
import numpy as np
from jax import lax

D = 2048
FF = 512
TOP = 8
MICRO = 8
TOK_MB = 16
SECTIONS = 2
EXPERTS = 16
TOKENS = 256
CAP = 10
N_EXPERT = 8
N_DP = 2


def levels(rng, extent, cuts, low, top_value):
    def one(dim, shards_of):
        heights = jax.random.uniform(jax.random.fold_in(jax.random.fold_in(rng, 6), dim), (shards_of,), jnp.float32, low / len(cuts), top_value / len(cuts))
        return jnp.repeat(jnp.exp(heights), extent[dim] // shards_of).reshape((-1,) + (1,) * (len(extent) - dim - 1))

    level = one(*cuts[0])
    for cut in cuts[1:]:
        level = level * one(*cut)
    return level


def shared_out(key, own, number, rows, amount, top, reach, skew):
    sequence = jax.random.permutation(key, amount)
    heavy_load, common = portions_of(amount, rows * top, reach, skew, True), portions_of(amount, rows * top, reach, skew, False)
    places = jnp.arange(amount)

    def named(lengths, turn):
        used = int((lengths > 0).sum())
        fixed = max(1, used // 4)
        passed = fixed + (places - fixed + turn * (used - fixed)) % max(1, amount - fixed)
        return jnp.zeros((amount,), jnp.int32).at[sequence[jnp.where(places < fixed, places, passed)]].set(jnp.asarray(lengths, jnp.int32))

    lengths = jnp.where(number % 4 == 0, named(heavy_load, number // 4), named(common, number - number // 4 - 1))
    mixed = jax.random.permutation(jax.random.fold_in(own, 3), amount)
    source_of, receiver = mixed[0:amount // 2 * 2:2], mixed[1:amount // 2 * 2:2]
    room = jnp.minimum(lengths[source_of] - 1, reach - lengths[receiver]) // 2
    room = jnp.where((source_of == sequence[0]) | (receiver == sequence[0]) | (lengths[receiver] == 0), 0, jnp.maximum(room, 0))
    passed = jax.random.randint(jax.random.fold_in(own, 4), (amount // 2,), 0, 1 << 20) % (room + 1)
    lengths = lengths.at[source_of].add(-passed).at[receiver].add(passed)
    items = jnp.searchsorted(jnp.cumsum(lengths), jnp.arange(rows * top), side="right").astype(jnp.int32)
    listing = items.reshape(top, rows).T
    listing = listing[jax.random.permutation(jax.random.fold_in(own, 1), rows)]
    turn = jax.random.randint(jax.random.fold_in(own, 2), (rows, 1), 0, top)
    return jnp.take_along_axis(listing, (jnp.arange(top)[None, :] + turn) % top, axis=1)


def portions_of(amount, total, reach, skew, full):
    portions = [(1 << 20) // math.isqrt(standing ** skew) + 1 for standing in range(1, amount + 1)]
    largest = reach if full else min(reach, max(-(-total // amount), total * portions[0] // sum(portions)))
    least = 1 if total - largest >= amount - 1 else 0
    given, rest = [largest] + [least] * (amount - 1), total - largest - least * (amount - 1)
    while rest > 0:
        candidates = [i for i in range(1, amount) if given[i] < largest] or [i for i in range(1, amount) if given[i] < reach]
        whole, left = sum([portions[i] for i in candidates]), rest
        for i in candidates:
            addition = min(reach - given[i], max(1, left * portions[i] // whole), rest)
            given[i] = given[i] + addition
            rest = rest - addition
    return np.array(given)


def bell_draw(key, dims, spread, bound, cuts=(), kind=jnp.bfloat16):
    level = levels(key, dims, cuts, -0.22, 0.18) if cuts else 1.0
    result = jax.random.normal(key, dims, jnp.float32) * spread * level
    return jnp.minimum(jnp.maximum(result, -bound), bound).astype(kind)


def setup_inputs(seed: int = 0) -> dict:
    splits = jax.random.split(jax.random.key(seed), 9)
    tokens_in = bell_draw(splits[0], (MICRO, TOKENS, D), 1.0, 6.0, ((1, 16),))
    cotangent = bell_draw(splits[1], (MICRO, TOKENS, D), 0.25, 4.0, ((1, 16),))
    routes_keys = jax.random.split(jax.random.fold_in(splits[2], 1), SECTIONS * MICRO * TOKENS // TOK_MB)
    routes_turns = jax.random.permutation(jax.random.fold_in(splits[2], 3), SECTIONS * MICRO * TOKENS // TOK_MB)
    routes = jax.vmap(lambda own, number: shared_out(jax.random.fold_in(splits[2], 2), own, number, TOK_MB, EXPERTS, TOP, CAP, 1))(routes_keys, routes_turns).reshape((SECTIONS, MICRO, TOKENS, TOP))
    router_weights = jnp.clip(jnp.exp(math.log(0.6) - 1.7917595 * jax.random.uniform(splits[3], (SECTIONS, MICRO, TOKENS, TOP), jnp.float32) ** levels(splits[3], (SECTIONS, MICRO, TOKENS, TOP), ((0, 2), (2, 16)), -0.2, 0.2)), 0.1, 0.6)
    norm_gain = jnp.clip(1.0 + 0.15 * jax.random.normal(splits[4], (SECTIONS, D), jnp.float32), 0.25, 1.75)
    w_gate = bell_draw(splits[5], (SECTIONS, EXPERTS, D, FF), D ** -0.5, 0.125, ((0, 2), (1, 8)))
    w_up = bell_draw(splits[6], (SECTIONS, EXPERTS, D, FF), D ** -0.5, 0.125, ((0, 2), (1, 8)))
    w_down = bell_draw(splits[7], (SECTIONS, EXPERTS, FF, D), FF ** -0.5, 0.25, ((0, 2), (1, 8)))
    return {"tokens_in": tokens_in, "cotangent": cotangent, "routes": routes, "router_weights": router_weights, "norm_gain": norm_gain, "w_gate": w_gate, "w_up": w_up, "w_down": w_down}


epsilon = 1e-06

def normalize(hidden, gain_row):
    widened = hidden.astype(jnp.float32)
    inv_rms = lax.rsqrt(lax.optimization_barrier(jnp.mean(widened * widened, axis=-1, keepdims=True)) + epsilon)
    return ((widened * inv_rms * gain_row).astype(jnp.bfloat16), widened, inv_rms)

def slot_rows(route_ids):
    blocks = N_EXPERT * N_DP
    per_block = TOK_MB * TOP
    grouped = route_ids.reshape(MICRO, blocks, per_block)
    labels = jnp.arange(EXPERTS, dtype=jnp.int32)
    onehot = (grouped[:, :, :, None] == labels).astype(jnp.int32)
    earlier = jnp.cumsum(onehot, axis=2) - onehot
    position = lax.optimization_barrier(jnp.sum(earlier * onehot, axis=3)).astype(jnp.int32)
    block_ids = jnp.arange(MICRO, dtype=jnp.int32)[:, None, None] * blocks + jnp.arange(blocks, dtype=jnp.int32)[None, :, None]
    expert_rows = MICRO * blocks * CAP
    flat_rows = grouped * expert_rows + block_ids * CAP + position
    return flat_rows.reshape(MICRO * TOKENS * TOP).astype(jnp.int32)

def source_table(flat_rows):
    total = MICRO * TOKENS * TOP
    expert_rows = MICRO * N_EXPERT * N_DP * CAP
    source = jnp.full((EXPERTS * expert_rows,), total, dtype=jnp.int32)
    source = source.at[flat_rows].set(jnp.arange(total, dtype=jnp.int32))
    return source.reshape(EXPERTS, expert_rows)

def layer_forward(hidden, route_ids, route_weights, gain_row, gate_w, up_w, down_w):
    normed, widened, inv_rms = normalize(hidden, gain_row)
    flat_rows = slot_rows(route_ids)
    source = source_table(flat_rows)
    padded = jnp.concatenate([normed.reshape(MICRO * TOKENS, D), jnp.zeros((1, D), jnp.bfloat16)], axis=0)

    def one_expert(inputs):
        picks, gate_m, up_m, down_m = inputs
        rows_in = padded[picks // TOP]
        gate_pre = jnp.dot(rows_in, gate_m, preferred_element_type=jnp.float32)
        up_pre = jnp.dot(rows_in, up_m, preferred_element_type=jnp.float32)
        act_value = (jax.nn.silu(gate_pre) * up_pre).astype(jnp.bfloat16)
        return jnp.dot(act_value, down_m, preferred_element_type=jnp.float32).astype(jnp.bfloat16)
    produced = lax.map(one_expert, (source, gate_w, up_w, down_w))
    gathered = produced.reshape(EXPERTS * source.shape[1], D)[flat_rows].astype(jnp.float32)
    gathered = gathered.reshape(MICRO, TOKENS, TOP, D)
    mixed_sum = widened + lax.optimization_barrier(jnp.sum(route_weights[:, :, :, None] * gathered, axis=2))
    return mixed_sum.astype(jnp.bfloat16)

def round_part(partial_value):
    return lax.optimization_barrier(partial_value.astype(jnp.bfloat16)).astype(jnp.float32)

def layer_backward(hidden, grad_out, route_ids, route_weights, gain_row, gate_w, up_w, down_w):
    normed, widened, inv_rms = normalize(hidden, gain_row)
    flat_rows = slot_rows(route_ids)
    source = source_table(flat_rows)
    total = MICRO * TOKENS * TOP
    padded = jnp.concatenate([normed.reshape(MICRO * TOKENS, D), jnp.zeros((1, D), jnp.bfloat16)], axis=0)
    spread_grad = route_weights.reshape(MICRO * TOKENS, TOP)[:, :, None] * grad_out.reshape(MICRO * TOKENS, 1, D).astype(jnp.float32)
    padded_grad = jnp.concatenate([spread_grad.astype(jnp.bfloat16).reshape(total, D), jnp.zeros((1, D), jnp.bfloat16)], axis=0)
    split_shape = (MICRO, N_EXPERT, N_DP, CAP)

    def one_expert(inputs):
        picks, gate_m, up_m, down_m = inputs
        rows_in = padded[picks // TOP]
        out_grad = padded_grad[picks]
        gate_pre = jnp.dot(rows_in, gate_m, preferred_element_type=jnp.float32)
        up_pre = jnp.dot(rows_in, up_m, preferred_element_type=jnp.float32)
        sigmoid_g = jax.nn.sigmoid(gate_pre)
        act_value = (jax.nn.silu(gate_pre) * up_pre).astype(jnp.bfloat16)
        act_grad = jnp.dot(out_grad, down_m.T, preferred_element_type=jnp.float32)
        up_grad = (act_grad * gate_pre * sigmoid_g).astype(jnp.bfloat16)
        gate_grad = (act_grad * up_pre * sigmoid_g * (1.0 + gate_pre * (1.0 - sigmoid_g))).astype(jnp.bfloat16)
        row_grad = (jnp.dot(gate_grad, gate_m.T, preferred_element_type=jnp.float32) + jnp.dot(up_grad, up_m.T, preferred_element_type=jnp.float32)).astype(jnp.bfloat16)
        rows_split = rows_in.reshape(split_shape + (D,))
        gate_split = gate_grad.reshape(split_shape + (FF,))
        up_split = up_grad.reshape(split_shape + (FF,))
        act_split = act_value.reshape(split_shape + (FF,))
        out_split = out_grad.reshape(split_shape + (D,))
        gate_total = jnp.zeros((D, FF), jnp.float32)
        up_total = jnp.zeros((D, FF), jnp.float32)
        down_total = jnp.zeros((FF, D), jnp.float32)
        for data_index in range(N_DP):
            part_rows = rows_split[:, :, data_index].reshape(-1, D)
            part_act = act_split[:, :, data_index].reshape(-1, FF)
            gate_total = gate_total + round_part(jnp.dot(part_rows.T, gate_split[:, :, data_index].reshape(-1, FF), preferred_element_type=jnp.float32))
            up_total = up_total + round_part(jnp.dot(part_rows.T, up_split[:, :, data_index].reshape(-1, FF), preferred_element_type=jnp.float32))
            down_total = down_total + round_part(jnp.dot(part_act.T, out_split[:, :, data_index].reshape(-1, D), preferred_element_type=jnp.float32))
        return (row_grad, gate_total.astype(jnp.bfloat16), up_total.astype(jnp.bfloat16), down_total.astype(jnp.bfloat16))
    row_grads, gate_grads, up_grads, down_grads = lax.map(one_expert, (source, gate_w, up_w, down_w))
    backed = row_grads.reshape(EXPERTS * source.shape[1], D)[flat_rows].astype(jnp.float32)
    dnormed = lax.optimization_barrier(jnp.sum(backed.reshape(MICRO, TOKENS, TOP, D), axis=2))
    scaled = dnormed * gain_row
    unit_rows = widened * inv_rms
    dhidden = grad_out.astype(jnp.float32) + inv_rms * (scaled - unit_rows * lax.optimization_barrier(jnp.mean(scaled * unit_rows, axis=-1, keepdims=True)))
    return (dhidden.astype(jnp.bfloat16), gate_grads, up_grads, down_grads)

def reference(tokens_in, cotangent, routes, router_weights, norm_gain, w_gate, w_up, w_down):
    hidden = tokens_in
    layer_inputs = []
    layer_outputs = []
    for layer_index in range(SECTIONS):
        layer_inputs.append(hidden)
        hidden = layer_forward(hidden, routes[layer_index], router_weights[layer_index], norm_gain[layer_index], w_gate[layer_index], w_up[layer_index], w_down[layer_index])
        layer_outputs.append(hidden)
    gradient = cotangent
    input_grads = [None] * SECTIONS
    gate_list = [None] * SECTIONS
    up_list = [None] * SECTIONS
    down_list = [None] * SECTIONS
    for layer_index in reversed(range(SECTIONS)):
        gradient, gate_part, up_part, down_part = layer_backward(layer_inputs[layer_index], gradient, routes[layer_index], router_weights[layer_index], norm_gain[layer_index], w_gate[layer_index], w_up[layer_index], w_down[layer_index])
        input_grads[layer_index] = gradient
        gate_list[layer_index] = gate_part
        up_list[layer_index] = up_part
        down_list[layer_index] = down_part
    return (jnp.stack(layer_outputs), jnp.stack(input_grads), jnp.stack(gate_list), jnp.stack(up_list), jnp.stack(down_list))
```

```python
import functools

import jax
import jax.numpy as jnp
from jax import lax
from jax.experimental import pallas as pl
from jax.experimental.pallas import tpu as pltpu
from jax.sharding import PartitionSpec as P

MESH = pl.DeviceIdType.MESH
F32, BF16 = jnp.float32, jnp.bfloat16
epsilon = 1e-06
CHUNK_ROWS = 256


def wait_in(ref, sem):
    pltpu.make_async_copy(ref, ref, sem).wait()


def step_kernel(
    sizes,
    tokens, cotangent, gain, table, w_gate, w_up, w_down,
    layer_out, input_grad, grad_gate, grad_up, grad_down,
    wg, wu, wd, dg, du, dd,
    rows_in, grads_in, pre_g, pre_u, act_s, gg_s, ug_s,
    hid, gout, tabs, spread,
    part_f, one_f, sum_f, two_f, part_b, one_b, sum_b, two_b,
    w_sem, o_sem, tab_s, tab_r, agf_s, agf_r, agb_s, agb_r,
    f1s, f1r, f2s, f2r, b1s, b1r, b2s, b2r,
    yf_s, yf_r, yb_s, yb_r, dp_s, dp_r, dp_free,
):
    S, E, nf, ns, ndp, C, r, D, held, FF = sizes
    inner = held * FF
    R = E * r
    s = lax.axis_index("section")
    e = lax.axis_index("expert")
    d = lax.axis_index("dp")
    sl, fa = e // nf, e % nf

    slow_peers = [(sl + k) % ns for k in range(1, ns)]
    fast_peers = [(fa + k) % nf for k in range(1, nf)]

    def send(src, dst, ss, rs, **where):
        return pltpu.make_async_remote_copy(
            src_ref=src, dst_ref=dst, send_sem=ss, recv_sem=rs, device_id=where, device_id_type=MESH
        )

    weight_copies = []
    for h in range(held):
        cols = pl.ds(h * FF, FF)
        weight_copies.append(pltpu.make_async_copy(w_gate.at[0, h], wg.at[:, cols], w_sem.at[0, h]))
        weight_copies.append(pltpu.make_async_copy(w_up.at[0, h], wu.at[:, cols], w_sem.at[1, h]))
        weight_copies.append(pltpu.make_async_copy(w_down.at[0, h], wd.at[cols], w_sem.at[2, h]))
    for copy in weight_copies:
        copy.start()

    barrier = pltpu.get_barrier_semaphore()
    greeted = [{"expert": q * nf + fa} for q in slow_peers]
    greeted += [{"expert": sl * nf + f} for f in fast_peers]
    greeted += [{"section": (s + k) % S} for k in ((1, S - 1) if S > 1 else ())]
    greeted += [{"dp": (d + k) % ndp} for k in range(1, ndp)]
    for where in greeted:
        pl.semaphore_signal(barrier, inc=1, device_id=where, device_id_type=MESH)
    pl.semaphore_wait(barrier, len(greeted))

    def gather_start(at, ss, rs):
        for f in fast_peers:
            send(at(e), at(e), ss.at[f, sl], rs.at[e], expert=sl * nf + f).start()
        for q in slow_peers:
            send(at(e), at(e), ss.at[nf, q], rs.at[e], expert=q * nf + fa).start()

    def gather_forward(at, ss, rs):
        for k in range(1, ns):
            p = (sl + ns - k) % ns
            block = p * nf + fa
            wait_in(at(block), rs.at[block])
            for f in fast_peers:
                send(at(block), at(block), ss.at[f, p], rs.at[block], expert=sl * nf + f).start()

    def gather_finish(at, ss, rs):
        for k in range(ns):
            p = (sl + ns - k) % ns
            for f in fast_peers:
                wait_in(at(p * nf + f), rs.at[p * nf + f])
        for q in slow_peers:
            wait_in(at(e), ss.at[nf, q])
        for k in range(ns):
            p = (sl + ns - k) % ns
            for f in fast_peers:
                wait_in(at(p * nf + fa), ss.at[f, p])

    def scatter_start(part, one, ss, rs):
        for k in range(1, ns + 1):
            q = (sl + k) % ns
            for f in fast_peers:
                send(part.at[q * nf + f], one.at[fa, q], ss.at[f, q], rs.at[fa, q], expert=sl * nf + f).start()

    def crossed(part, one, q):
        total = part[q * nf + fa].astype(F32)
        for f in fast_peers:
            total = total + one[f, q].astype(F32)
        return total

    def scatter_middle(part, one, rs, summed, two, ss2, rs2):
        for k in range(1, ns + 1):
            q = (sl + k) % ns
            for f in fast_peers:
                wait_in(one.at[f, q], rs.at[f, q])
            if k < ns:
                summed[q] = crossed(part, one, q).astype(BF16)
                send(summed.at[q], two.at[sl], ss2.at[q], rs2.at[sl], expert=q * nf + fa).start()

    def scatter_finish(part, one, ss, summed, two, ss2, rs2):
        total = crossed(part, one, sl)
        for k in range(1, ns):
            p = (sl + ns - k) % ns
            wait_in(two.at[p], rs2.at[p])
            total = total + two[p].astype(F32)
        for k in range(1, ns + 1):
            q = (sl + k) % ns
            for f in fast_peers:
                wait_in(part.at[q * nf + f], ss.at[f, q])
            if k < ns:
                wait_in(summed.at[q], ss2.at[q])
        return total

    def normalizer(c):
        widened = hid[c].astype(F32)
        return widened, lax.rsqrt(jnp.mean(widened * widened, axis=-1, keepdims=True) + epsilon)

    def active(c):
        return jnp.logical_and(c >= 0, c < C)

    def start_forward_gather(c):
        @pl.when(active(c))
        def _():
            @pl.when(s == 0)
            def _():
                hid[c] = tokens[c]

            @pl.when(s > 0)
            def _():
                wait_in(hid.at[c], yf_r.at[c])

            widened, inv_rms = normalizer(c)
            rows_in[c, e] = (widened * inv_rms * gain[...]).astype(BF16)
            gather_start(lambda b: rows_in.at[c, b], agf_s, agf_r)

    def whole(value, width):
        return jnp.concatenate([value] * (width // value.shape[1]), axis=1)

    experts = held * E
    tabs[e] = table[...]
    gather_start(lambda b: tabs.at[b], tab_s, tab_r)
    start_forward_gather(0 - s)
    gather_forward(lambda b: tabs.at[b], tab_s, tab_r)
    gather_finish(lambda b: tabs.at[b], tab_s, tab_r)
    for b in range(E):
        turned = tabs[b].T
        lanes = lax.broadcasted_iota(jnp.int32, turned.shape, 1)
        for h in range(held):
            column = jnp.sum(jnp.where(lanes == e * held + h, turned, 0.0), axis=1, keepdims=True)
            wide = jnp.broadcast_to(column, (turned.shape[0], 128))
            for c in range(C):
                spread[c, h, b * r : (b + 1) * r, :] = wide[c * r : (c + 1) * r]
    for copy in weight_copies:
        copy.wait()

    def forward_compute(c):
        rows = rows_in[c].reshape(R, D)
        for h in range(held):
            cols = pl.ds(h * FF, FF)
            gate = jnp.dot(rows, wg[:, cols], preferred_element_type=F32).astype(BF16)
            up = jnp.dot(rows, wu[:, cols], preferred_element_type=F32).astype(BF16)
            pre_g[c, :, cols] = gate
            pre_u[c, :, cols] = up
            gate, up = gate.astype(F32), up.astype(F32)
            act_s[:, cols] = (gate * jax.nn.sigmoid(gate) * up * whole(spread[c, h], FF)).astype(BF16)
        mixed = jnp.dot(act_s[...], wd[...], preferred_element_type=F32)
        part_f[...] = mixed.astype(BF16).reshape(E, r, D)

    nt = (((1,), (1,)), ((), ()))
    tn = (((0,), (0,)), ((), ()))

    def backward_compute(c, slot):
        grads = grads_in[slot].reshape(R, D)
        for h in range(held):
            cols = pl.ds(h * FF, FF)
            act_grad = lax.dot_general(grads, wd[cols], nt, preferred_element_type=F32)
            weight = whole(spread[c, h], FF)
            act_grad = act_grad * weight
            gate, up = pre_g[c, :, cols].astype(F32), pre_u[c, :, cols].astype(F32)
            sig = jax.nn.sigmoid(gate)
            act_s[:, cols] = (gate * sig * up * weight).astype(BF16)
            gg_s[:, cols] = (act_grad * up * sig * (1.0 + gate * (1.0 - sig))).astype(BF16)
            ug_s[:, cols] = (act_grad * gate * sig).astype(BF16)
        row_grad = lax.dot_general(gg_s[...], wg[...], nt, preferred_element_type=F32)
        row_grad = row_grad + lax.dot_general(ug_s[...], wu[...], nt, preferred_element_type=F32)
        part_b[...] = row_grad.astype(BF16).reshape(E, r, D)

    def weight_grads(c, slot):
        tile = 256

        def add(total, rows, value):
            old = jnp.where(c == 0, 0.0, total[rows].astype(F32))
            total[rows] = (old + value).astype(BF16)

        def in_tile(i, carry):
            rows = pl.ds(pl.multiple_of(i * tile, tile), tile)
            left = rows_in[c, :, :, rows].reshape(R, tile)
            add(dg, rows, lax.dot_general(left, gg_s[...], tn, preferred_element_type=F32))
            add(du, rows, lax.dot_general(left, ug_s[...], tn, preferred_element_type=F32))
            return carry

        def out_tile(i, carry):
            rows = pl.ds(pl.multiple_of(i * tile, tile), tile)
            right = grads_in[slot].reshape(R, D)
            add(dd, rows, lax.dot_general(act_s[:, rows], right, tn, preferred_element_type=F32))
            return carry

        lax.fori_loop(0, D // tile, in_tile, 0)
        lax.fori_loop(0, inner // tile, out_tile, 0)

    def tick_body(tick, carry):
        cf = tick - s
        cb = tick - (2 * (S - 1) - s)
        on_f, on_b = active(cf), active(cb)
        slot = (cb + 2 * S) % 2

        def fwd(b):
            return rows_in.at[cf, b]

        def bwd(b):
            return grads_in.at[slot, b]

        @pl.when(on_f)
        def _():
            gather_finish(fwd, agf_s, agf_r)

        @pl.when(on_b)
        def _():
            @pl.when(s == S - 1)
            def _():
                gout[cb] = cotangent[cb]

            @pl.when(s < S - 1)
            def _():
                wait_in(gout.at[cb], yb_r.at[cb])

            grads_in[slot, e] = gout[cb]
            gather_start(bwd, agb_s, agb_r)

        @pl.when(on_f)
        def _():
            forward_compute(cf)
            scatter_start(part_f, one_f, f1s, f1r)

        @pl.when(on_b)
        def _():
            gather_forward(bwd, agb_s, agb_r)

        @pl.when(on_f)
        def _():
            scatter_middle(part_f, one_f, f1r, sum_f, two_f, f2s, f2r)

        @pl.when(on_b)
        def _():
            gather_finish(bwd, agb_s, agb_r)

        @pl.when(on_f)
        def _():
            total = scatter_finish(part_f, one_f, f1s, sum_f, two_f, f2s, f2r)
            layer_out[cf] = (hid[cf].astype(F32) + total).astype(BF16)

            @pl.when(s < S - 1)
            def _():
                send(layer_out.at[cf], hid.at[cf], yf_s.at[cf], yf_r.at[cf], section=(s + 1) % S).start()

        start_forward_gather(cf + 1)

        @pl.when(on_b)
        def _():
            backward_compute(cb, slot)
            scatter_start(part_b, one_b, b1s, b1r)

        @pl.when(active(cf + 1))
        def _():
            gather_forward(lambda b: rows_in.at[cf + 1, b], agf_s, agf_r)

        @pl.when(on_b)
        def _():
            scatter_middle(part_b, one_b, b1r, sum_b, two_b, b2s, b2r)
            weight_grads(cb, slot)
            total = scatter_finish(part_b, one_b, b1s, sum_b, two_b, b2s, b2r)
            widened, inv_rms = normalizer(cb)
            unit = widened * inv_rms
            scaled = total * gain[...]
            centre = jnp.mean(scaled * unit, axis=-1, keepdims=True)
            input_grad[cb] = (gout[cb].astype(F32) + inv_rms * (scaled - unit * centre)).astype(BF16)

            @pl.when(s > 0)
            def _():
                send(input_grad.at[cb], gout.at[cb], yb_s.at[cb], yb_r.at[cb], section=(s + S - 1) % S).start()

        return carry

    @pl.when(active(0 - s))
    def _():
        gather_forward(lambda b: rows_in.at[0 - s, b], agf_s, agf_r)

    lax.fori_loop(0, C + 2 * (S - 1), tick_body, 0)

    def drain(c, carry):
        @pl.when(s < S - 1)
        def _():
            wait_in(layer_out.at[c], yf_s.at[c])

        @pl.when(s > 0)
        def _():
            wait_in(input_grad.at[c], yb_s.at[c])

        return carry

    lax.fori_loop(0, C, drain, 0)

    others = [(d + k) % ndp for k in range(1, ndp)]
    for other in others:
        pl.semaphore_signal(dp_free, inc=1, device_id={"dp": other}, device_id_type=MESH)
    pl.semaphore_wait(dp_free, ndp - 1)
    rows_d, rows_f = D // ndp, FF // ndp
    moved = []
    for k in range(1, ndp):
        other = (d + k) % ndp
        theirs = pl.ds(pl.multiple_of(other * rows_d, rows_d), rows_d)
        land = pl.ds((k - 1) * rows_d, rows_d)
        moved.append(send(dg.at[theirs], wg.at[land], dp_s.at[0, k], dp_r.at[0, k], dp=other))
        moved.append(send(du.at[theirs], wu.at[land], dp_s.at[1, k], dp_r.at[1, k], dp=other))
        for h in range(held):
            theirs = pl.ds(pl.multiple_of(h * FF + other * rows_f, rows_f), rows_f)
            land = pl.ds(((k - 1) * held + h) * rows_f, rows_f)
            moved.append(send(dd.at[theirs], wd.at[land], dp_s.at[2 + h, k], dp_r.at[2 + h, k], dp=other))
    for copy in moved:
        copy.start()
    for copy in moved:
        copy.wait()
    outs = []
    tile = 256

    def fold(total, base, landing, starts, count):
        def body(i, carry):
            rows = pl.ds(pl.multiple_of(base + i * tile, tile), tile)
            value = total[rows].astype(F32)
            for start in starts:
                value = value + landing[pl.ds(pl.multiple_of(start + i * tile, tile), tile)].astype(F32)
            total[rows] = value.astype(BF16)
            return carry

        lax.fori_loop(0, count // tile, body, 0)

    base = pl.multiple_of(d * rows_d, rows_d)
    for index, (total, landing, out) in enumerate(((dg, wg, grad_gate), (du, wu, grad_up))):
        fold(total, base, landing, [k * rows_d for k in range(ndp - 1)], rows_d)
        for h in range(held):
            copy = pltpu.make_async_copy(
                total.at[pl.ds(base, rows_d), pl.ds(h * FF, FF)], out.at[0, h], o_sem.at[index, h]
            )
            copy.start()
            outs.append(copy)
    for h in range(held):
        base = pl.multiple_of(h * FF + d * rows_f, rows_f)
        fold(dd, base, wd, [(k * held + h) * rows_f for k in range(ndp - 1)], rows_f)
        copy = pltpu.make_async_copy(dd.at[pl.ds(base, rows_f)], grad_down.at[0, h], o_sem.at[2, h])
        copy.start()
        outs.append(copy)
    for copy in outs:
        copy.wait()


def on_device(tokens_in, cotangent, routes, router_weights, norm_gain, w_gate, w_up, w_down):
    micro, rows, D = tokens_in.shape
    held, FF = w_gate.shape[1], w_gate.shape[3]
    S, E, ndp = lax.axis_size("section"), lax.axis_size("expert"), lax.axis_size("dp")
    nf = 1
    while E % (4 * nf * nf) == 0:
        nf *= 2
    ns = E // nf
    C = 1
    while micro % (2 * C) == 0 and micro * rows * E > CHUNK_ROWS * C:
        C *= 2
    r = micro * rows // C
    R = E * r
    inner = held * FF
    experts = held * E
    own = micro * rows

    labels = jnp.arange(experts, dtype=jnp.int32)[:, None, None]
    named = routes.reshape(1, own, routes.shape[-1])
    given = router_weights.reshape(1, own, routes.shape[-1])
    table = jnp.sum(jnp.where(named == labels, given, 0.0), axis=2)

    vmem, dma = pltpu.VMEM, pltpu.SemaphoreType.DMA
    scratch = [
        vmem((D, inner), BF16), vmem((D, inner), BF16), vmem((inner, D), BF16),
        vmem((D, inner), BF16), vmem((D, inner), BF16), vmem((inner, D), BF16),
        vmem((C, E, r, D), BF16), vmem((2, E, r, D), BF16),
        vmem((C, R, inner), BF16), vmem((C, R, inner), BF16),
        vmem((R, inner), BF16), vmem((R, inner), BF16), vmem((R, inner), BF16),
        vmem((C, r, D), BF16), vmem((C, r, D), BF16),
        vmem((E, experts, own), F32), vmem((C, held, R, 128), F32),
    ]
    for _ in range(2):
        scratch += [
            vmem((E, r, D), BF16), vmem((nf, ns, r, D), BF16), vmem((ns, r, D), BF16), vmem((ns, r, D), BF16)
        ]
    scratch += [dma((3, held)), dma((3, held))]
    for _ in range(3):
        scratch += [dma((nf + 1, ns)), dma((E,))]
    for _ in range(2):
        scratch += [dma((nf, ns)), dma((nf, ns)), dma((ns,)), dma((ns,))]
    scratch += [dma((C,))] * 4
    scratch += [dma((2 + held, ndp)), dma((2 + held, ndp)), pltpu.SemaphoreType.REGULAR]

    in_vmem, anywhere = pl.BlockSpec(memory_space=pltpu.VMEM), pl.BlockSpec(memory_space=pl.ANY)
    outs = pl.pallas_call(
        functools.partial(step_kernel, (S, E, nf, ns, ndp, C, r, D, held, FF)),
        out_shape=(
            jax.ShapeDtypeStruct((C, r, D), BF16),
            jax.ShapeDtypeStruct((C, r, D), BF16),
            jax.ShapeDtypeStruct((1, held, D // ndp, FF), BF16),
            jax.ShapeDtypeStruct((1, held, D // ndp, FF), BF16),
            jax.ShapeDtypeStruct((1, held, FF // ndp, D), BF16),
        ),
        in_specs=[in_vmem] * 4 + [anywhere] * 3,
        out_specs=(in_vmem, in_vmem, anywhere, anywhere, anywhere),
        scratch_shapes=scratch,
        compiler_params=pltpu.CompilerParams(
            collective_id=0, has_side_effects=True, vmem_limit_bytes=67_000_000
        ),
    )(
        tokens_in.reshape(C, r, D), cotangent.reshape(C, r, D), norm_gain, table, w_gate, w_up, w_down
    )
    layer_out, input_grad, grad_gate, grad_up, grad_down = outs
    shape = (1, micro, rows, D)
    return layer_out.reshape(shape), input_grad.reshape(shape), grad_gate, grad_up, grad_down


def solution(mesh):
    placed = (
        P(None, ("expert", "dp"), None),
        P(None, ("expert", "dp"), None),
        P("section", None, ("expert", "dp"), None),
        P("section", None, ("expert", "dp"), None),
        P("section", None),
        P("section", "expert", None, None),
        P("section", "expert", None, None),
        P("section", "expert", None, None),
    )
    return jax.shard_map(
        on_device,
        mesh=mesh,
        in_specs=placed,
        out_specs=(
            P("section", None, ("expert", "dp"), None),
            P("section", None, ("expert", "dp"), None),
            P("section", "expert", "dp", None),
            P("section", "expert", "dp", None),
            P("section", "expert", "dp", None),
        ),
        check_vma=False,
    )
```

```python
import functools

import jax
import jax.numpy as jnp
from jax import lax
from jax.experimental import pallas as pl
from jax.experimental.pallas import tpu as pltpu
from jax.sharding import PartitionSpec as P

MESH = pl.DeviceIdType.MESH
F32, BF16 = jnp.float32, jnp.bfloat16
epsilon = 1e-06
CHUNK_ROWS = 256


def wait_in(ref, sem):
    pltpu.make_async_copy(ref, ref, sem).wait()


def step_kernel(
    sizes,
    tokens, cotangent, gain, table, w_gate, w_up, w_down,
    layer_out, input_grad, grad_gate, grad_up, grad_down,
    wg, wu, wd, dg, du, dd,
    rows_in, grads_in, pre_g, pre_u, act_s, gg_s, ug_s,
    hid, gout, out_f, out_b, tabs, spread,
    part_f, one_f, sum_f, two_f, part_b, one_b, sum_b, two_b,
    w_sem, o_sem, tab_s, tab_r, agf_s, agf_r, agb_s, agb_r,
    f1s, f1r, f2s, f2r, b1s, b1r, b2s, b2r,
    yf_s, yf_r, yb_s, yb_r, hf_sem, hb_sem, dp_s, dp_r, dp_free,
):
    S, E, nf, ns, ndp, C, r, D, held, FF = sizes
    inner = held * FF
    R = E * r
    s = lax.axis_index("section")
    e = lax.axis_index("expert")
    d = lax.axis_index("dp")
    sl, fa = e // nf, e % nf

    slow_peers = [(sl + k) % ns for k in range(1, ns)]
    fast_peers = [(fa + k) % nf for k in range(1, nf)]

    def send(src, dst, ss, rs, **where):
        return pltpu.make_async_remote_copy(
            src_ref=src, dst_ref=dst, send_sem=ss, recv_sem=rs, device_id=where, device_id_type=MESH
        )

    weight_copies = []
    for h in range(held):
        cols = pl.ds(h * FF, FF)
        weight_copies.append(pltpu.make_async_copy(w_gate.at[0, h], wg.at[:, cols], w_sem.at[0, h]))
        weight_copies.append(pltpu.make_async_copy(w_up.at[0, h], wu.at[:, cols], w_sem.at[1, h]))
        weight_copies.append(pltpu.make_async_copy(w_down.at[0, h], wd.at[cols], w_sem.at[2, h]))
    for copy in weight_copies:
        copy.start()

    barrier = pltpu.get_barrier_semaphore()
    greeted = [{"expert": q * nf + fa} for q in slow_peers]
    greeted += [{"expert": sl * nf + f} for f in fast_peers]
    greeted += [{"section": (s + k) % S} for k in ((1, S - 1) if S > 1 else ())]
    greeted += [{"dp": (d + k) % ndp} for k in range(1, ndp)]
    for where in greeted:
        pl.semaphore_signal(barrier, inc=1, device_id=where, device_id_type=MESH)
    pl.semaphore_wait(barrier, len(greeted))

    def gather_start(at, ss, rs):
        for f in fast_peers:
            send(at(e), at(e), ss.at[f, sl], rs.at[e], expert=sl * nf + f).start()
        for q in slow_peers:
            send(at(e), at(e), ss.at[nf, q], rs.at[e], expert=q * nf + fa).start()

    def gather_forward(at, ss, rs):
        for k in range(1, ns):
            p = (sl + ns - k) % ns
            block = p * nf + fa
            wait_in(at(block), rs.at[block])
            for f in fast_peers:
                send(at(block), at(block), ss.at[f, p], rs.at[block], expert=sl * nf + f).start()

    def gather_finish(at, ss, rs):
        for k in range(ns):
            p = (sl + ns - k) % ns
            for f in fast_peers:
                wait_in(at(p * nf + f), rs.at[p * nf + f])
        for q in slow_peers:
            wait_in(at(e), ss.at[nf, q])
        for k in range(ns):
            p = (sl + ns - k) % ns
            for f in fast_peers:
                wait_in(at(p * nf + fa), ss.at[f, p])

    def scatter_start(part, one, ss, rs):
        for k in range(1, ns + 1):
            q = (sl + k) % ns
            for f in fast_peers:
                send(part.at[q * nf + f], one.at[fa, q], ss.at[f, q], rs.at[fa, q], expert=sl * nf + f).start()

    def crossed(part, one, q):
        total = part[q * nf + fa].astype(F32)
        for f in fast_peers:
            total = total + one[f, q].astype(F32)
        return total

    def scatter_middle(part, one, rs, summed, two, ss2, rs2):
        for k in range(1, ns + 1):
            q = (sl + k) % ns
            for f in fast_peers:
                wait_in(one.at[f, q], rs.at[f, q])
            if k < ns:
                summed[q] = crossed(part, one, q).astype(BF16)
                send(summed.at[q], two.at[sl], ss2.at[q], rs2.at[sl], expert=q * nf + fa).start()

    def scatter_finish(part, one, ss, summed, two, ss2, rs2):
        total = crossed(part, one, sl)
        for k in range(1, ns):
            p = (sl + ns - k) % ns
            wait_in(two.at[p], rs2.at[p])
            total = total + two[p].astype(F32)
        for k in range(1, ns + 1):
            q = (sl + k) % ns
            for f in fast_peers:
                wait_in(part.at[q * nf + f], ss.at[f, q])
            if k < ns:
                wait_in(summed.at[q], ss2.at[q])
        return total

    def normalizer(c):
        widened = hid[c].astype(F32)
        return widened, lax.rsqrt(jnp.mean(widened * widened, axis=-1, keepdims=True) + epsilon)

    def active(c):
        return jnp.logical_and(c >= 0, c < C)

    def start_forward_gather(c):
        @pl.when(active(c))
        def _():
            @pl.when(s == 0)
            def _():
                hid[c] = tokens[c]

            @pl.when(s > 0)
            def _():
                wait_in(hid.at[c], yf_r.at[c])

            widened, inv_rms = normalizer(c)
            rows_in[c, e] = (widened * inv_rms * gain[...]).astype(BF16)
            gather_start(lambda b: rows_in.at[c, b], agf_s, agf_r)

    def whole(value, width):
        return jnp.concatenate([value] * (width // value.shape[1]), axis=1)

    experts = held * E
    tabs[e] = table[...]
    gather_start(lambda b: tabs.at[b], tab_s, tab_r)
    start_forward_gather(0 - s)
    gather_forward(lambda b: tabs.at[b], tab_s, tab_r)
    gather_finish(lambda b: tabs.at[b], tab_s, tab_r)
    for b in range(E):
        turned = tabs[b].T
        lanes = lax.broadcasted_iota(jnp.int32, turned.shape, 1)
        for h in range(held):
            column = jnp.sum(jnp.where(lanes == e * held + h, turned, 0.0), axis=1, keepdims=True)
            wide = jnp.broadcast_to(column, (turned.shape[0], 128))
            for c in range(C):
                spread[c, h, b * r : (b + 1) * r, :] = wide[c * r : (c + 1) * r]
    for copy in weight_copies:
        copy.wait()

    def forward_compute(c):
        rows = rows_in[c].reshape(R, D)
        for h in range(held):
            cols = pl.ds(h * FF, FF)
            gate = jnp.dot(rows, wg[:, cols], preferred_element_type=F32).astype(BF16)
            up = jnp.dot(rows, wu[:, cols], preferred_element_type=F32).astype(BF16)
            pre_g[c, :, cols] = gate
            pre_u[c, :, cols] = up
            gate, up = gate.astype(F32), up.astype(F32)
            act_s[:, cols] = (gate * jax.nn.sigmoid(gate) * up * whole(spread[c, h], FF)).astype(BF16)
        mixed = jnp.dot(act_s[...], wd[...], preferred_element_type=F32)
        part_f[...] = mixed.astype(BF16).reshape(E, r, D)

    nt = (((1,), (1,)), ((), ()))
    tn = (((0,), (0,)), ((), ()))

    def backward_compute(c, slot):
        grads = grads_in[slot].reshape(R, D)
        for h in range(held):
            cols = pl.ds(h * FF, FF)
            act_grad = lax.dot_general(grads, wd[cols], nt, preferred_element_type=F32)
            weight = whole(spread[c, h], FF)
            act_grad = act_grad * weight
            gate, up = pre_g[c, :, cols].astype(F32), pre_u[c, :, cols].astype(F32)
            sig = jax.nn.sigmoid(gate)
            act_s[:, cols] = (gate * sig * up * weight).astype(BF16)
            gg_s[:, cols] = (act_grad * up * sig * (1.0 + gate * (1.0 - sig))).astype(BF16)
            ug_s[:, cols] = (act_grad * gate * sig).astype(BF16)
        row_grad = lax.dot_general(gg_s[...], wg[...], nt, preferred_element_type=F32)
        row_grad = row_grad + lax.dot_general(ug_s[...], wu[...], nt, preferred_element_type=F32)
        part_b[...] = row_grad.astype(BF16).reshape(E, r, D)

    def weight_grads(c, slot):
        tile = 256

        def add(total, rows, value):
            old = jnp.where(c == 0, 0.0, total[rows].astype(F32))
            total[rows] = (old + value).astype(BF16)

        def in_tile(i, carry):
            rows = pl.ds(pl.multiple_of(i * tile, tile), tile)
            left = rows_in[c, :, :, rows].reshape(R, tile)
            add(dg, rows, lax.dot_general(left, gg_s[...], tn, preferred_element_type=F32))
            add(du, rows, lax.dot_general(left, ug_s[...], tn, preferred_element_type=F32))
            return carry

        def out_tile(i, carry):
            rows = pl.ds(pl.multiple_of(i * tile, tile), tile)
            right = grads_in[slot].reshape(R, D)
            add(dd, rows, lax.dot_general(act_s[:, rows], right, tn, preferred_element_type=F32))
            return carry

        lax.fori_loop(0, D // tile, in_tile, 0)
        lax.fori_loop(0, inner // tile, out_tile, 0)

    rows_d, rows_f = D // ndp, FF // ndp

    def dp_copies():
        moved = []
        for k in range(1, ndp):
            other = (d + k) % ndp
            theirs = pl.ds(pl.multiple_of(other * rows_d, rows_d), rows_d)
            land = pl.ds((k - 1) * rows_d, rows_d)
            moved.append(send(dg.at[theirs], wg.at[land], dp_s.at[0, k], dp_r.at[0, k], dp=other))
            moved.append(send(du.at[theirs], wu.at[land], dp_s.at[1, k], dp_r.at[1, k], dp=other))
            for h in range(held):
                theirs = pl.ds(pl.multiple_of(h * FF + other * rows_f, rows_f), rows_f)
                land = pl.ds(((k - 1) * held + h) * rows_f, rows_f)
                moved.append(send(dd.at[theirs], wd.at[land], dp_s.at[2 + h, k], dp_r.at[2 + h, k], dp=other))
        return moved

    def dp_start():
        for k in range(1, ndp):
            pl.semaphore_signal(dp_free, inc=1, device_id={"dp": (d + k) % ndp}, device_id_type=MESH)
        pl.semaphore_wait(dp_free, ndp - 1)
        for copy in dp_copies():
            copy.start()

    def tick_body(tick, carry):
        cf = tick - s
        cb = tick - (2 * (S - 1) - s)
        on_f, on_b = active(cf), active(cb)
        slot = (cb + 2 * S) % 2

        def fwd(b):
            return rows_in.at[cf, b]

        def bwd(b):
            return grads_in.at[slot, b]

        @pl.when(on_f)
        def _():
            gather_finish(fwd, agf_s, agf_r)

        @pl.when(on_b)
        def _():
            @pl.when(s == S - 1)
            def _():
                gout[cb] = cotangent[cb]

            @pl.when(s < S - 1)
            def _():
                wait_in(gout.at[cb], yb_r.at[cb])

            grads_in[slot, e] = gout[cb]
            gather_start(bwd, agb_s, agb_r)

        @pl.when(on_f)
        def _():
            forward_compute(cf)
            scatter_start(part_f, one_f, f1s, f1r)

        @pl.when(on_b)
        def _():
            gather_forward(bwd, agb_s, agb_r)

        @pl.when(on_f)
        def _():
            scatter_middle(part_f, one_f, f1r, sum_f, two_f, f2s, f2r)

        @pl.when(on_b)
        def _():
            gather_finish(bwd, agb_s, agb_r)

        @pl.when(on_f)
        def _():
            total = scatter_finish(part_f, one_f, f1s, sum_f, two_f, f2s, f2r)
            out_f[cf] = (hid[cf].astype(F32) + total).astype(BF16)
            pltpu.make_async_copy(out_f.at[cf], layer_out.at[cf], hf_sem.at[cf]).start()

            @pl.when(s < S - 1)
            def _():
                send(out_f.at[cf], hid.at[cf], yf_s.at[cf], yf_r.at[cf], section=(s + 1) % S).start()

        start_forward_gather(cf + 1)

        @pl.when(on_b)
        def _():
            backward_compute(cb, slot)
            scatter_start(part_b, one_b, b1s, b1r)

        @pl.when(active(cf + 1))
        def _():
            gather_forward(lambda b: rows_in.at[cf + 1, b], agf_s, agf_r)

        @pl.when(on_b)
        def _():
            scatter_middle(part_b, one_b, b1r, sum_b, two_b, b2s, b2r)
            weight_grads(cb, slot)
            pl.when(jnp.logical_and(cb == C - 1, s == 0))(dp_start)
            total = scatter_finish(part_b, one_b, b1s, sum_b, two_b, b2s, b2r)
            widened, inv_rms = normalizer(cb)
            unit = widened * inv_rms
            scaled = total * gain[...]
            centre = jnp.mean(scaled * unit, axis=-1, keepdims=True)
            out_b[cb] = (gout[cb].astype(F32) + inv_rms * (scaled - unit * centre)).astype(BF16)
            pltpu.make_async_copy(out_b.at[cb], input_grad.at[cb], hb_sem.at[cb]).start()

            @pl.when(s > 0)
            def _():
                send(out_b.at[cb], gout.at[cb], yb_s.at[cb], yb_r.at[cb], section=(s + S - 1) % S).start()

        pl.when(jnp.logical_and(cb == C - 1, s > 0))(dp_start)
        return carry

    @pl.when(active(0 - s))
    def _():
        gather_forward(lambda b: rows_in.at[0 - s, b], agf_s, agf_r)

    lax.fori_loop(0, C + 2 * (S - 1), tick_body, 0)

    def drain(c, carry):
        wait_in(out_f.at[c], hf_sem.at[c])
        wait_in(out_b.at[c], hb_sem.at[c])

        @pl.when(s < S - 1)
        def _():
            wait_in(out_f.at[c], yf_s.at[c])

        @pl.when(s > 0)
        def _():
            wait_in(out_b.at[c], yb_s.at[c])

        return carry

    lax.fori_loop(0, C, drain, 0)

    for copy in dp_copies():
        copy.wait()
    outs = []
    tile = 256

    def fold(total, base, landing, starts, count):
        def body(i, carry):
            rows = pl.ds(pl.multiple_of(base + i * tile, tile), tile)
            value = total[rows].astype(F32)
            for start in starts:
                value = value + landing[pl.ds(pl.multiple_of(start + i * tile, tile), tile)].astype(F32)
            total[rows] = value.astype(BF16)
            return carry

        lax.fori_loop(0, count // tile, body, 0)

    base = pl.multiple_of(d * rows_d, rows_d)
    for index, (total, landing, out) in enumerate(((dg, wg, grad_gate), (du, wu, grad_up))):
        fold(total, base, landing, [k * rows_d for k in range(ndp - 1)], rows_d)
        for h in range(held):
            copy = pltpu.make_async_copy(
                total.at[pl.ds(base, rows_d), pl.ds(h * FF, FF)], out.at[0, h], o_sem.at[index, h]
            )
            copy.start()
            outs.append(copy)
    for h in range(held):
        base = pl.multiple_of(h * FF + d * rows_f, rows_f)
        fold(dd, base, wd, [(k * held + h) * rows_f for k in range(ndp - 1)], rows_f)
        copy = pltpu.make_async_copy(dd.at[pl.ds(base, rows_f)], grad_down.at[0, h], o_sem.at[2, h])
        copy.start()
        outs.append(copy)
    for copy in outs:
        copy.wait()


def on_device(tokens_in, cotangent, routes, router_weights, norm_gain, w_gate, w_up, w_down):
    micro, rows, D = tokens_in.shape
    held, FF = w_gate.shape[1], w_gate.shape[3]
    S, E, ndp = lax.axis_size("section"), lax.axis_size("expert"), lax.axis_size("dp")
    nf = 1
    while E % (4 * nf * nf) == 0:
        nf *= 2
    ns = E // nf
    C = 1
    while micro % (2 * C) == 0 and micro * rows * E > CHUNK_ROWS * C:
        C *= 2
    r = micro * rows // C
    R = E * r
    inner = held * FF
    experts = held * E
    own = micro * rows

    labels = jnp.arange(experts, dtype=jnp.int32)[:, None, None]
    named = routes.reshape(1, own, routes.shape[-1])
    given = router_weights.reshape(1, own, routes.shape[-1])
    table = jnp.sum(jnp.where(named == labels, given, 0.0), axis=2)

    vmem, dma = pltpu.VMEM, pltpu.SemaphoreType.DMA
    scratch = [
        vmem((D, inner), BF16), vmem((D, inner), BF16), vmem((inner, D), BF16),
        vmem((D, inner), BF16), vmem((D, inner), BF16), vmem((inner, D), BF16),
        vmem((C, E, r, D), BF16), vmem((2, E, r, D), BF16),
        vmem((C, R, inner), BF16), vmem((C, R, inner), BF16),
        vmem((R, inner), BF16), vmem((R, inner), BF16), vmem((R, inner), BF16),
        vmem((C, r, D), BF16), vmem((C, r, D), BF16), vmem((C, r, D), BF16), vmem((C, r, D), BF16),
        vmem((E, experts, own), F32), vmem((C, held, R, 128), F32),
    ]
    for _ in range(2):
        scratch += [
            vmem((E, r, D), BF16), vmem((nf, ns, r, D), BF16), vmem((ns, r, D), BF16), vmem((ns, r, D), BF16)
        ]
    scratch += [dma((3, held)), dma((3, held))]
    for _ in range(3):
        scratch += [dma((nf + 1, ns)), dma((E,))]
    for _ in range(2):
        scratch += [dma((nf, ns)), dma((nf, ns)), dma((ns,)), dma((ns,))]
    scratch += [dma((C,))] * 6
    scratch += [dma((2 + held, ndp)), dma((2 + held, ndp)), pltpu.SemaphoreType.REGULAR]

    in_vmem, anywhere = pl.BlockSpec(memory_space=pltpu.VMEM), pl.BlockSpec(memory_space=pl.ANY)
    outs = pl.pallas_call(
        functools.partial(step_kernel, (S, E, nf, ns, ndp, C, r, D, held, FF)),
        out_shape=(
            jax.ShapeDtypeStruct((C, r, D), BF16),
            jax.ShapeDtypeStruct((C, r, D), BF16),
            jax.ShapeDtypeStruct((1, held, D // ndp, FF), BF16),
            jax.ShapeDtypeStruct((1, held, D // ndp, FF), BF16),
            jax.ShapeDtypeStruct((1, held, FF // ndp, D), BF16),
        ),
        in_specs=[in_vmem] * 4 + [anywhere] * 3,
        out_specs=(anywhere,) * 5,
        scratch_shapes=scratch,
        compiler_params=pltpu.CompilerParams(
            collective_id=0, has_side_effects=True, vmem_limit_bytes=67_000_000
        ),
    )(
        tokens_in.reshape(C, r, D), cotangent.reshape(C, r, D), norm_gain, table, w_gate, w_up, w_down
    )
    layer_out, input_grad, grad_gate, grad_up, grad_down = outs
    shape = (1, micro, rows, D)
    return layer_out.reshape(shape), input_grad.reshape(shape), grad_gate, grad_up, grad_down


def solution(mesh):
    placed = (
        P(None, ("expert", "dp"), None),
        P(None, ("expert", "dp"), None),
        P("section", None, ("expert", "dp"), None),
        P("section", None, ("expert", "dp"), None),
        P("section", None),
        P("section", "expert", None, None),
        P("section", "expert", None, None),
        P("section", "expert", None, None),
    )
    return jax.shard_map(
        on_device,
        mesh=mesh,
        in_specs=placed,
        out_specs=(
            P("section", None, ("expert", "dp"), None),
            P("section", None, ("expert", "dp"), None),
            P("section", "expert", "dp", None),
            P("section", "expert", "dp", None),
            P("section", "expert", "dp", None),
        ),
        check_vma=False,
    )
```
